1024 devices in a mesh: blk: 32 (over z_lo, x), freq: 32 (over z_hi, y, core).
Axes of the slice: x: 4, y: 4, z: 32 (z_hi: 4, z_lo: 8; z = z_hi * 8 + z_lo), core: 2. Of those that a mesh axis runs over, the one named last changes fastest.
Arguments:
- shot_rows: bfloat16 [2, 32, 256, 4096], P(None, 'freq', None, 'blk'), may hold values from -6 to 6
- surface_op: bfloat16 [2, 32, 4096, 4096], P(None, 'freq', None, 'blk'), may hold values from -0.09375 to 0.09375
- aperture: int32 [32, 32, 32], P('freq', None, 'blk'), may hold values from 0 to 1, as said below
Outputs:
- traces: float32 [256, 16, 4096], P('freq', None, 'blk')
The draws below stay inside these ranges and needn't reach their ends.
Inputs may be any that keep to these rules, and one draw needn't show every extreme that they name: aperture[f, b, b] is 1 for every f and b.
All inputs are finite; a program needn't handle non-finite values.
Results may differ from the reference program's by a relative error of at most 0.0003.
Values may be sent and summed in bfloat16 or wider, within the bound.
No kernel may reach another device: no remote copies, remote signals or barrier semaphores. Data moves between devices by JAX's collectives and lax.ppermute only.
A program may use at most 32 MiB of HBM per device.

```python
import math
import jax
import jax.numpy as jnp
from jax import lax

BLOCK = 128
NT = 16
PERIOD = 4096
BINS = 2048
BLOCKS = 32
K = 4096
SHOTS = 256
FREQS = 32


def draw_aperture(key, part):
    first, second = jax.random.split(key)
    reach = jax.random.randint(first, (FREQS, 1, BLOCKS), 0, BLOCKS // 2 + 1)
    ladder = jnp.arange(BLOCKS, dtype=jnp.int32)
    spread = jnp.abs(ladder[:, None] - ladder[None, :])
    distance = jnp.minimum(spread, BLOCKS - spread)[None, :, :]
    chosen = jax.random.randint(second, (FREQS, BLOCKS, BLOCKS), 0, 4) > 0
    inside = (distance == 0) | (distance <= reach) & chosen
    return jnp.where(inside, 1, 0).astype(jnp.int32)


def level_of(own_key, extent, shards, least, top_value):
    gain, own = 1.0, jax.random.fold_in(own_key, 6)
    for position, shards_of in shards:
        steps = jnp.exp(jax.random.uniform(jax.random.fold_in(own, position), (shards_of,), jnp.float32, least / len(shards), top_value / len(shards)))
        gain = gain * jnp.repeat(steps, extent[position] // shards_of).reshape([-1 if axis == position else 1 for axis in range(len(extent))])
    return gain


def centred(own_key, extent, scale, limit, pieces=(), kind=jnp.bfloat16):
    loudness = level_of(own_key, extent, pieces, -0.22, 0.18) if pieces else 1.0
    drawn = jax.random.normal(own_key, extent, jnp.float32) * scale * loudness
    return jnp.minimum(jnp.maximum(drawn, -limit), limit).astype(kind)


def setup_inputs(seed: int = 0) -> dict:
    seeds = jax.random.split(jax.random.key(seed), 4)
    shot_rows = centred(seeds[0], (2, FREQS, SHOTS, K), 1.0, 6.0, ((1, 32), (3, 32)))
    surface_op = centred(seeds[1], (2, FREQS, K, K), K ** -0.5, 0.09375, ((1, 32), (3, 32)))
    aperture = draw_aperture(jax.random.fold_in(seeds[3], 71), 0)
    return dict(shot_rows=shot_rows, surface_op=surface_op, aperture=aperture)


def tables():
    slices = jnp.arange(FREQS, dtype=jnp.int32)
    bins = 1 + slices * (BINS // FREQS)
    times = jnp.arange(NT, dtype=jnp.int32)
    phase = bins[:, None] * times[None, :] % PERIOD
    theta = 2.0 * math.pi * phase.astype(jnp.float32) / PERIOD
    return (jnp.cos(theta), jnp.sin(theta))

def reference(shot_rows, surface_op, aperture):
    cosine_table, sine_table = tables()
    scale = 1.0 / math.sqrt(FREQS)
    input_spectra = shot_rows.astype(jnp.float32)
    upper_bound = lax.Precision.HIGHEST

    def one_block(index):
        start = (index * BLOCK).astype(jnp.int32)
        block_op = lax.dynamic_slice_in_dim(surface_op, start, BLOCK, 3).astype(jnp.float32)
        column = lax.dynamic_index_in_dim(aperture, index, 2, keepdims=False)
        keep = jnp.repeat(column, BLOCK, axis=1).astype(jnp.float32)
        masked_blocks = block_op * keep[None, :, :, None]
        real_values = jnp.einsum('wzx,wxu->wzu', input_spectra[0], masked_blocks[0], precision=upper_bound) - jnp.einsum('wzx,wxu->wzu', input_spectra[1], masked_blocks[1], precision=upper_bound)
        imaginary_values = jnp.einsum('wzx,wxu->wzu', input_spectra[0], masked_blocks[1], precision=upper_bound) + jnp.einsum('wzx,wxu->wzu', input_spectra[1], masked_blocks[0], precision=upper_bound)
        output_traces = jnp.einsum('hd,hki->kdi', cosine_table, real_values, precision=upper_bound) - jnp.einsum('hd,hki->kdi', sine_table, imaginary_values, precision=upper_bound)
        return output_traces * scale
    blocks_out = lax.map(one_block, jnp.arange(BLOCKS, dtype=jnp.int32))
    return jnp.transpose(blocks_out, (1, 2, 0, 3)).reshape(SHOTS, NT, K)
```

```python
import math

import jax
import jax.numpy as jnp
import numpy as np
from jax import lax
from jax.sharding import Mesh, PartitionSpec as P

NT = 16
PERIOD = 4096
BINS = 2048
ZL, NX, ZH, NY, NC = 8, 4, 4, 4, 2
BLK = ("zl", "x")
FREQ = ("zh", "y", "c")


def transform_matrix(total):
    bins = 1 + np.arange(total) * (BINS // total)
    phase = bins[:, None] * np.arange(NT)[None, :] % PERIOD
    theta = (2.0 * math.pi * phase.astype(np.float32) / PERIOD).astype(np.float32)
    scale = 1.0 / math.sqrt(total)
    return np.stack([np.cos(theta) * scale, -np.sin(theta) * scale]).astype(np.float32)


def shift(value, step):
    return lax.ppermute(value, "x", [(i, (i + step) % NX) for i in range(NX)])


def per_device(shot_rows, surface_op, aperture):
    x = lax.axis_index("x")
    width = surface_op.shape[3]
    shots = shot_rows.shape[2]
    total = ZH * NY * NC

    rows = surface_op.reshape(2, ZL, NX, width, width)
    keep = aperture.reshape(ZL, NX).astype(jnp.bfloat16)

    def quarter(owner):
        part = lax.dynamic_index_in_dim(rows, owner, 2, keepdims=False)
        mask = lax.dynamic_index_in_dim(keep, owner, 1, keepdims=False)
        return part * mask[None, :, None, None]

    ops = [quarter(x)] + [shift(quarter((x + d) % NX), d) for d in (1, 3, 2)]
    own = shot_rows.reshape(2, shots, width)
    copies = jnp.broadcast_to(own[None], (ZL,) + own.shape)
    gathered = lax.all_to_all(copies, "zl", 0, 0, tiled=True)

    def product(op):
        wide = jnp.einsum("zpsk,qzkr->pqsr", gathered, op, preferred_element_type=jnp.float32)
        return jnp.stack([wide[0, 0] - wide[1, 1], wide[0, 1] + wide[1, 0]])

    spectra = product(ops[0])
    for d, op in zip((1, 3, 2), ops[1:]):
        spectra = spectra + shift(product(op), -d)

    mine = lax.all_to_all(
        spectra.reshape(2, total, shots // total, width), FREQ, 1, 1, tiled=True
    )
    return jnp.einsum(
        "pft,pfsr->str",
        jnp.asarray(transform_matrix(total)),
        mine,
        precision=lax.Precision.HIGHEST,
    )


def solution(mesh):
    fine = Mesh(
        mesh.devices.reshape(ZL, NX, ZH, NY, NC), BLK + FREQ
    )
    return jax.shard_map(
        per_device,
        mesh=fine,
        in_specs=(
            P(None, FREQ, None, BLK),
            P(None, FREQ, None, BLK),
            P(FREQ, None, BLK),
        ),
        out_specs=P(FREQ, None, BLK),
        check_vma=False,
    )
```

```python
import math

import jax
import jax.numpy as jnp
import numpy as np
from jax import lax
from jax.experimental import pallas as pl
from jax.experimental.pallas import tpu as pltpu
from jax.sharding import Mesh, PartitionSpec as P

NT = 16
PERIOD = 4096
BINS = 2048
ZQ, ZR, NX, ZH, NY, NC = 2, 4, 4, 4, 4, 2
BLK = ("zq", "zr", "x")
FREQ = ("zh", "y", "c")


def transform_matrix(total):
    bins = 1 + np.arange(total) * (BINS // total)
    phase = bins[:, None] * np.arange(NT)[None, :] % PERIOD
    theta = (2.0 * math.pi * phase.astype(np.float32) / PERIOD).astype(np.float32)
    scale = 1.0 / math.sqrt(total)
    return np.stack([np.cos(theta) * scale, -np.sin(theta) * scale]).astype(np.float32)


def product_kernel(place_ref, *refs):
    near_refs, (far_ref, op_ref, out_ref, rows_ref) = refs[:ZR], refs[ZR:]
    shots, width = far_ref.shape[2:]

    @pl.when(pl.program_id(0) == 0)
    def _():
        for part in range(2):
            for z in range(ZR):
                at = pl.ds(part * shots, shots)
                rows_ref[at, z * width : (z + 1) * width] = near_refs[z][part]
                rows_ref[at, (ZR + z) * width : (ZR + z + 1) * width] = far_ref[z, part]

    quad, mine = place_ref[0], place_ref[1]
    order = [quad * ZR + (mine ^ d) for d in range(ZR)]
    order += [(1 - quad) * ZR + z for z in range(ZR)]
    op = jnp.concatenate(
        [jnp.concatenate([op_ref[0, 0, z], op_ref[0, 1, z]], axis=1) for z in order], axis=0
    )
    wide = jnp.dot(rows_ref[...], op, preferred_element_type=jnp.float32)
    out_ref[0, 0] = wide[:shots, :width] - wide[shots:, width:]
    out_ref[0, 1] = wide[:shots, width:] + wide[shots:, :width]


def product(place, near, far, op):
    shots, width = far.shape[2:]
    depth = 2 * ZR * width
    return pl.pallas_call(
        product_kernel,
        out_shape=jax.ShapeDtypeStruct((NX, 2, shots, width), jnp.float32),
        grid_spec=pltpu.PrefetchScalarGridSpec(
            num_scalar_prefetch=1,
            grid=(NX,),
            in_specs=[pl.BlockSpec((2, shots, width), lambda i, q: (0, 0, 0))] * ZR
            + [
                pl.BlockSpec((ZR, 2, shots, width), lambda i, q: (0, 0, 0, 0)),
                pl.BlockSpec((1, 2, 2 * ZR, width, width), lambda i, q: (i, 0, 0, 0, 0)),
            ],
            out_specs=pl.BlockSpec((1, 2, shots, width), lambda i, q: (i, 0, 0, 0)),
            scratch_shapes=[pltpu.VMEM((2 * shots, depth), jnp.bfloat16)],
        ),
        compiler_params=pltpu.CompilerParams(vmem_limit_bytes=16 << 20),
        cost_estimate=pl.CostEstimate(
            flops=2 * NX * 2 * shots * depth * 2 * width,
            bytes_accessed=6 << 20,
            transcendentals=0,
        ),
    )(place, *near, far, op)


def per_device(shot_rows, surface_op, aperture):
    width = surface_op.shape[3]
    shots = shot_rows.shape[2]
    total = ZH * NY * NC
    place = jnp.stack([lax.axis_index("zq"), lax.axis_index("zr")]).astype(jnp.int32)

    own = shot_rows.reshape(2, shots, width)
    crossed = lax.ppermute(own, "zq", [(0, 1), (1, 0)])

    keep = aperture.reshape(ZQ * ZR, NX).astype(jnp.bfloat16)
    rows = surface_op.reshape(2, ZQ * ZR, NX, width, width) * keep[None, :, :, None, None]
    op = lax.all_to_all(jnp.transpose(rows, (2, 0, 1, 3, 4)), "x", 0, 0, tiled=True)

    near = [own] + [
        lax.ppermute(own, "zr", [(i, i ^ d) for i in range(ZR)]) for d in range(1, ZR)
    ]
    far = lax.all_gather(crossed, "zr", axis=0)

    parts = lax.all_to_all(product(place, near, far, op), "x", 0, 0, tiled=True)
    spectra = (parts[0] + parts[1]) + (parts[2] + parts[3])
    sent = jnp.transpose(spectra.reshape(2, total, shots // total, width), (1, 0, 2, 3))
    mine = lax.all_to_all(sent, FREQ, 0, 0, tiled=True)
    return jnp.einsum(
        "pft,fpsr->str",
        jnp.asarray(transform_matrix(total)),
        mine,
        precision=lax.Precision.HIGHEST,
    )


def solution(mesh):
    fine = Mesh(mesh.devices.reshape(ZQ, ZR, NX, ZH, NY, NC), BLK + FREQ)
    return jax.shard_map(
        per_device,
        mesh=fine,
        in_specs=(
            P(None, FREQ, None, BLK),
            P(None, FREQ, None, BLK),
            P(FREQ, None, BLK),
        ),
        out_specs=P(FREQ, None, BLK),
        check_vma=False,
    )
```

```python
import math

import jax
import jax.numpy as jnp
import numpy as np
from jax import lax
from jax.experimental import pallas as pl
from jax.experimental.pallas import tpu as pltpu
from jax.sharding import Mesh, PartitionSpec as P

NT = 16
PERIOD = 4096
BINS = 2048
ZQ, ZR, NX, ZH, NY, NC = 2, 4, 4, 4, 4, 2
BLK = ("zq", "zr", "x")
FREQ = ("zh", "y", "c")


def transform_matrix(total):
    bins = 1 + np.arange(total) * (BINS // total)
    phase = bins[:, None] * np.arange(NT)[None, :] % PERIOD
    theta = (2.0 * math.pi * phase.astype(np.float32) / PERIOD).astype(np.float32)
    scale = 1.0 / math.sqrt(total)
    return np.stack([np.cos(theta) * scale, -np.sin(theta) * scale]).astype(np.float32)


def product_kernel(place_ref, *refs):
    near_refs, (far_ref, op_ref, out_ref, rows_ref) = refs[:ZR], refs[ZR:]
    shots, width = far_ref.shape[2:]

    @pl.when(pl.program_id(0) == 0)
    def _():
        for part in range(2):
            for z in range(ZR):
                at = pl.ds(part * shots, shots)
                rows_ref[at, z * width : (z + 1) * width] = near_refs[z][part]
                rows_ref[at, (ZR + z) * width : (ZR + z + 1) * width] = far_ref[z, part]

    quad, mine = place_ref[0], place_ref[1]
    order = [quad * ZR + (mine ^ d) for d in range(ZR)]
    order += [(1 - quad) * ZR + z for z in range(ZR)]
    op = jnp.concatenate(
        [jnp.concatenate([op_ref[0, 0, z], op_ref[0, 1, z]], axis=1) for z in order], axis=0
    )
    wide = jnp.dot(rows_ref[...], op, preferred_element_type=jnp.float32)
    out_ref[0, 0] = wide[:shots, :width] - wide[shots:, width:]
    out_ref[0, 1] = wide[:shots, width:] + wide[shots:, :width]


def product(place, near, far, op):
    shots, width = far.shape[2:]
    depth = 2 * ZR * width
    return pl.pallas_call(
        product_kernel,
        out_shape=jax.ShapeDtypeStruct((NX, 2, shots, width), jnp.float32),
        grid_spec=pltpu.PrefetchScalarGridSpec(
            num_scalar_prefetch=1,
            grid=(NX,),
            in_specs=[pl.BlockSpec((2, shots, width), lambda i, q: (0, 0, 0))] * ZR
            + [
                pl.BlockSpec((ZR, 2, shots, width), lambda i, q: (0, 0, 0, 0)),
                pl.BlockSpec((1, 2, 2 * ZR, width, width), lambda i, q: (i, 0, 0, 0, 0)),
            ],
            out_specs=pl.BlockSpec((1, 2, shots, width), lambda i, q: (i, 0, 0, 0)),
            scratch_shapes=[pltpu.VMEM((2 * shots, depth), jnp.bfloat16)],
        ),
        compiler_params=pltpu.CompilerParams(vmem_limit_bytes=16 << 20),
        cost_estimate=pl.CostEstimate(
            flops=2 * NX * 2 * shots * depth * 2 * width,
            bytes_accessed=6 << 20,
            transcendentals=0,
        ),
    )(place, *near, far, op)


def per_device(shot_rows, surface_op, aperture):
    width = surface_op.shape[3]
    shots = shot_rows.shape[2]
    total = ZH * NY * NC
    place = jnp.stack([lax.axis_index("zq"), lax.axis_index("zr")]).astype(jnp.int32)

    own = shot_rows.reshape(2, shots, width)
    crossed = lax.ppermute(own, "zq", [(0, 1), (1, 0)])

    keep = aperture.reshape(ZQ * ZR, NX).astype(jnp.bfloat16)
    rows = surface_op.reshape(2, ZQ * ZR, NX, width, width) * keep[None, :, :, None, None]
    op = lax.all_to_all(jnp.transpose(rows, (2, 0, 1, 3, 4)), "x", 0, 0, tiled=True)

    near = [own] + [
        lax.ppermute(own, "zr", [(i, i ^ d) for i in range(ZR)]) for d in range(1, ZR)
    ]
    far = lax.all_gather(crossed, "zr", axis=0)

    parts = lax.all_to_all(product(place, near, far, op), "x", 0, 0, tiled=True)
    spectra = (parts[0] + parts[1]) + (parts[2] + parts[3])
    peak = jnp.maximum(jnp.max(jnp.abs(spectra)), 2.0**-100)
    level = jnp.floor(jnp.log2(peak))
    sent = jnp.transpose(spectra.reshape(2, total, shots // total, width), (1, 0, 2, 3))
    sent = (sent * jnp.exp2(13.0 - level)).astype(jnp.float16)
    sent = jnp.concatenate(
        [
            sent.reshape(total, shots // total, 2, width),
            jnp.full((total, 1, 2, width), level, jnp.float16),
        ],
        axis=1,
    )
    mine = lax.all_to_all(sent, FREQ, 0, 0, tiled=True).astype(jnp.float32)
    values = mine[:, :-1].reshape(total, 2, shots // total, width)
    mine = values * jnp.exp2(mine[:, -1, 0] - 13.0)[:, None, None, :]
    return jnp.einsum(
        "pft,fpsr->str",
        jnp.asarray(transform_matrix(total)),
        mine,
        precision=lax.Precision.HIGHEST,
    )


def solution(mesh):
    fine = Mesh(mesh.devices.reshape(ZQ, ZR, NX, ZH, NY, NC), BLK + FREQ)
    return jax.shard_map(
        per_device,
        mesh=fine,
        in_specs=(
            P(None, FREQ, None, BLK),
            P(None, FREQ, None, BLK),
            P(FREQ, None, BLK),
        ),
        out_specs=P(FREQ, None, BLK),
        check_vma=False,
    )
```

```python
import math

import jax
import jax.numpy as jnp
import numpy as np
from jax import lax
from jax.experimental import pallas as pl
from jax.experimental.pallas import tpu as pltpu
from jax.sharding import Mesh, PartitionSpec as P

NT = 16
PERIOD = 4096
BINS = 2048
ZQ, ZR, NX, ZH, NY, NC = 2, 4, 4, 4, 4, 2
BLK = ("zq", "zr", "x")
FREQ = ("zh", "y", "c")


def transform_matrix(total):
    bins = 1 + np.arange(total) * (BINS // total)
    phase = bins[:, None] * np.arange(NT)[None, :] % PERIOD
    theta = (2.0 * math.pi * phase.astype(np.float32) / PERIOD).astype(np.float32)
    scale = 1.0 / math.sqrt(total)
    return np.stack([np.cos(theta) * scale, -np.sin(theta) * scale]).astype(np.float32)


def product_kernel(place_ref, *refs):
    near_refs, (far_ref, op_ref, out_ref, rows_ref) = refs[:ZR], refs[ZR:]
    shots, width = far_ref.shape[2:]

    @pl.when(pl.program_id(0) == 0)
    def _():
        for part in range(2):
            for z in range(ZR):
                at = pl.ds(part * shots, shots)
                rows_ref[at, z * width : (z + 1) * width] = near_refs[z][part]
                rows_ref[at, (ZR + z) * width : (ZR + z + 1) * width] = far_ref[z, part]

    quad, mine = place_ref[0], place_ref[1]
    order = [quad * ZR + (mine ^ d) for d in range(ZR)]
    order += [(1 - quad) * ZR + z for z in range(ZR)]
    op = jnp.concatenate(
        [jnp.concatenate([op_ref[0, 0, z], op_ref[0, 1, z]], axis=1) for z in order], axis=0
    )
    wide = jnp.dot(rows_ref[...], op, preferred_element_type=jnp.float32)
    out_ref[0, 0] = wide[:shots, :width] - wide[shots:, width:]
    out_ref[0, 1] = wide[:shots, width:] + wide[shots:, :width]


def product(place, near, far, op):
    shots, width = far.shape[2:]
    depth = 2 * ZR * width
    return pl.pallas_call(
        product_kernel,
        out_shape=jax.ShapeDtypeStruct((NX, 2, shots, width), jnp.float32),
        grid_spec=pltpu.PrefetchScalarGridSpec(
            num_scalar_prefetch=1,
            grid=(NX,),
            in_specs=[pl.BlockSpec((2, shots, width), lambda i, q: (0, 0, 0))] * ZR
            + [
                pl.BlockSpec((ZR, 2, shots, width), lambda i, q: (0, 0, 0, 0)),
                pl.BlockSpec((1, 2, 2 * ZR, width, width), lambda i, q: (i, 0, 0, 0, 0)),
            ],
            out_specs=pl.BlockSpec((1, 2, shots, width), lambda i, q: (i, 0, 0, 0)),
            scratch_shapes=[pltpu.VMEM((2 * shots, depth), jnp.bfloat16)],
        ),
        compiler_params=pltpu.CompilerParams(vmem_limit_bytes=16 << 20),
        cost_estimate=pl.CostEstimate(
            flops=2 * NX * 2 * shots * depth * 2 * width,
            bytes_accessed=6 << 20,
            transcendentals=0,
        ),
    )(place, *near, far, op)


def mask_kernel(keep_ref, rows_ref, out_ref, taken, masked, load_sems, store_sems):
    count = rows_ref.shape[1]
    loads = [
        pltpu.make_async_copy(rows_ref.at[:, z], taken.at[z], load_sems.at[z])
        for z in range(count)
    ]
    stores = [
        pltpu.make_async_copy(masked.at[z], out_ref.at[:, :, z], store_sems.at[z])
        for z in range(count)
    ]
    for load in loads:
        load.start()
    for z in range(count):
        loads[z].wait()
        for x in range(NX):
            keep = keep_ref[z * NX + x].astype(jnp.float32).astype(jnp.bfloat16)
            for part in range(2):
                masked[z, x, part] = taken[z, part, x] * keep
        stores[z].start()
    for store in stores:
        store.wait()


def masked_rows(keep, rows):
    parts, count, _, width, _ = rows.shape
    return pl.pallas_call(
        mask_kernel,
        out_shape=jax.ShapeDtypeStruct((NX, parts, count, width, width), rows.dtype),
        in_specs=[
            pl.BlockSpec(memory_space=pltpu.SMEM),
            pl.BlockSpec(memory_space=pltpu.HBM),
        ],
        out_specs=pl.BlockSpec(memory_space=pltpu.HBM),
        scratch_shapes=[
            pltpu.VMEM((count, parts, NX, width, width), rows.dtype),
            pltpu.VMEM((count, NX, parts, width, width), rows.dtype),
            pltpu.SemaphoreType.DMA((count,)),
            pltpu.SemaphoreType.DMA((count,)),
        ],
        compiler_params=pltpu.CompilerParams(vmem_limit_bytes=60 << 20),
        cost_estimate=pl.CostEstimate(
            flops=rows.size, bytes_accessed=4 * rows.size, transcendentals=0
        ),
    )(keep, rows)


def per_device(shot_rows, surface_op, aperture):
    width = surface_op.shape[3]
    shots = shot_rows.shape[2]
    total = ZH * NY * NC
    place = jnp.stack([lax.axis_index("zq"), lax.axis_index("zr")]).astype(jnp.int32)

    own = shot_rows.reshape(2, shots, width)
    crossed = lax.ppermute(own, "zq", [(0, 1), (1, 0)])

    rows = masked_rows(aperture.reshape(-1), surface_op.reshape(2, ZQ * ZR, NX, width, width))
    op = lax.all_to_all(rows, "x", 0, 0, tiled=True)

    near = [own] + [
        lax.ppermute(own, "zr", [(i, i ^ d) for i in range(ZR)]) for d in range(1, ZR)
    ]
    far = lax.all_gather(crossed, "zr", axis=0)

    parts = lax.all_to_all(product(place, near, far, op), "x", 0, 0, tiled=True)
    spectra = (parts[0] + parts[1]) + (parts[2] + parts[3])
    peak = jnp.maximum(jnp.max(jnp.abs(spectra)), 2.0**-100)
    level = jnp.floor(jnp.log2(peak))
    sent = jnp.transpose(spectra.reshape(2, total, shots // total, width), (1, 0, 2, 3))
    sent = (sent * jnp.exp2(13.0 - level)).astype(jnp.float16)
    sent = jnp.concatenate(
        [
            sent.reshape(total, shots // total, 2, width),
            jnp.full((total, 1, 2, width), level, jnp.float16),
        ],
        axis=1,
    )
    mine = lax.all_to_all(sent, FREQ, 0, 0, tiled=True).astype(jnp.float32)
    values = mine[:, :-1].reshape(total, 2, shots // total, width)
    mine = values * jnp.exp2(mine[:, -1, 0] - 13.0)[:, None, None, :]
    return jnp.einsum(
        "pft,fpsr->str",
        jnp.asarray(transform_matrix(total)),
        mine,
        precision=lax.Precision.HIGHEST,
    )


def solution(mesh):
    fine = Mesh(mesh.devices.reshape(ZQ, ZR, NX, ZH, NY, NC), BLK + FREQ)
    return jax.shard_map(
        per_device,
        mesh=fine,
        in_specs=(
            P(None, FREQ, None, BLK),
            P(None, FREQ, None, BLK),
            P(FREQ, None, BLK),
        ),
        out_specs=P(FREQ, None, BLK),
        check_vma=False,
    )
```

```python
import math

import jax
import jax.numpy as jnp
import numpy as np
from jax import lax
from jax.experimental import pallas as pl
from jax.experimental.pallas import tpu as pltpu
from jax.sharding import Mesh, PartitionSpec as P

NT = 16
PERIOD = 4096
BINS = 2048
ZQ, ZR, NX, ZH, NY, NC = 2, 4, 4, 4, 4, 2
BLK = ("zq", "zr", "x")
FREQ = ("zh", "y", "c")


def transform_matrix(total):
    bins = 1 + np.arange(total) * (BINS // total)
    phase = bins[:, None] * np.arange(NT)[None, :] % PERIOD
    theta = (2.0 * math.pi * phase.astype(np.float32) / PERIOD).astype(np.float32)
    scale = 1.0 / math.sqrt(total)
    return np.stack([np.cos(theta) * scale, -np.sin(theta) * scale]).astype(np.float32)


def product_kernel(place_ref, *refs):
    near_refs, (far_ref, op_ref, out_ref, rows_ref) = refs[:ZR], refs[ZR:]
    shots, width = far_ref.shape[2:]

    @pl.when(pl.program_id(0) == 0)
    def _():
        for part in range(2):
            for z in range(ZR):
                at = pl.ds(part * shots, shots)
                rows_ref[at, z * width : (z + 1) * width] = near_refs[z][part]
                rows_ref[at, (ZR + z) * width : (ZR + z + 1) * width] = far_ref[z, part]

    quad, mine = place_ref[0], place_ref[1]
    order = [quad * ZR + (mine ^ d) for d in range(ZR)]
    order += [(1 - quad) * ZR + z for z in range(ZR)]
    op = jnp.concatenate(
        [jnp.concatenate([op_ref[0, 0, z], op_ref[0, 1, z]], axis=1) for z in order], axis=0
    )
    wide = jnp.dot(rows_ref[...], op, preferred_element_type=jnp.float32)
    groups = (-1,) + out_ref.shape[3:]
    out_ref[0, :, 0] = (wide[:shots, :width] - wide[shots:, width:]).reshape(groups)
    out_ref[0, :, 1] = (wide[:shots, width:] + wide[shots:, :width]).reshape(groups)


def product(place, near, far, op, total):
    shots, width = far.shape[2:]
    groups = (total, 2, shots // total, width)
    depth = 2 * ZR * width
    return pl.pallas_call(
        product_kernel,
        out_shape=jax.ShapeDtypeStruct((NX,) + groups, jnp.float32),
        grid_spec=pltpu.PrefetchScalarGridSpec(
            num_scalar_prefetch=1,
            grid=(NX,),
            in_specs=[pl.BlockSpec((2, shots, width), lambda i, q: (0, 0, 0))] * ZR
            + [
                pl.BlockSpec((ZR, 2, shots, width), lambda i, q: (0, 0, 0, 0)),
                pl.BlockSpec((1, 2, 2 * ZR, width, width), lambda i, q: (i, 0, 0, 0, 0)),
            ],
            out_specs=pl.BlockSpec((1,) + groups, lambda i, q: (i, 0, 0, 0, 0)),
            scratch_shapes=[pltpu.VMEM((2 * shots, depth), jnp.bfloat16)],
        ),
        compiler_params=pltpu.CompilerParams(vmem_limit_bytes=16 << 20),
        cost_estimate=pl.CostEstimate(
            flops=2 * NX * 2 * shots * depth * 2 * width,
            bytes_accessed=6 << 20,
            transcendentals=0,
        ),
    )(place, *near, far, op)


def mask_kernel(keep_ref, rows_ref, out_ref, taken, masked, load_sems, store_sems):
    count = rows_ref.shape[1]
    loads = [
        pltpu.make_async_copy(rows_ref.at[:, z], taken.at[z], load_sems.at[z])
        for z in range(count)
    ]
    stores = [
        pltpu.make_async_copy(masked.at[z], out_ref.at[:, :, z], store_sems.at[z])
        for z in range(count)
    ]
    for load in loads:
        load.start()
    for z in range(count):
        loads[z].wait()
        for x in range(NX):
            keep = keep_ref[z * NX + x].astype(jnp.float32).astype(jnp.bfloat16)
            for part in range(2):
                masked[z, x, part] = taken[z, part, x] * keep
        stores[z].start()
    for store in stores:
        store.wait()


def masked_rows(keep, rows):
    parts, count, _, width, _ = rows.shape
    return pl.pallas_call(
        mask_kernel,
        out_shape=jax.ShapeDtypeStruct((NX, parts, count, width, width), rows.dtype),
        in_specs=[
            pl.BlockSpec(memory_space=pltpu.SMEM),
            pl.BlockSpec(memory_space=pltpu.HBM),
        ],
        out_specs=pl.BlockSpec(memory_space=pltpu.HBM),
        scratch_shapes=[
            pltpu.VMEM((count, parts, NX, width, width), rows.dtype),
            pltpu.VMEM((count, NX, parts, width, width), rows.dtype),
            pltpu.SemaphoreType.DMA((count,)),
            pltpu.SemaphoreType.DMA((count,)),
        ],
        compiler_params=pltpu.CompilerParams(vmem_limit_bytes=60 << 20),
        cost_estimate=pl.CostEstimate(
            flops=rows.size, bytes_accessed=4 * rows.size, transcendentals=0
        ),
    )(keep, rows)


def per_device(shot_rows, surface_op, aperture):
    width = surface_op.shape[3]
    shots = shot_rows.shape[2]
    total = ZH * NY * NC
    place = jnp.stack([lax.axis_index("zq"), lax.axis_index("zr")]).astype(jnp.int32)

    own = shot_rows.reshape(2, shots, width)
    crossed = lax.ppermute(own, "zq", [(0, 1), (1, 0)])

    rows = masked_rows(aperture.reshape(-1), surface_op.reshape(2, ZQ * ZR, NX, width, width))
    op = lax.all_to_all(rows, "x", 0, 0, tiled=True)

    near = [own] + [
        lax.ppermute(own, "zr", [(i, i ^ d) for i in range(ZR)]) for d in range(1, ZR)
    ]
    far = lax.all_gather(crossed, "zr", axis=0)

    parts = lax.all_to_all(product(place, near, far, op, total), "x", 0, 0, tiled=True)
    spectra = (parts[0] + parts[1]) + (parts[2] + parts[3])
    peak = jnp.maximum(jnp.max(jnp.abs(spectra)), 2.0**-100)
    level = jnp.floor(jnp.log2(peak))
    sent = (spectra * jnp.exp2(13.0 - level)).astype(jnp.float16)
    sent = jnp.concatenate(
        [
            sent.reshape(total, shots // total, 2, width),
            jnp.full((total, 1, 2, width), level, jnp.float16),
        ],
        axis=1,
    )
    mine = lax.all_to_all(sent, FREQ, 0, 0, tiled=True).astype(jnp.float32)
    values = mine[:, :-1].reshape(total, 2, shots // total, width)
    mine = values * jnp.exp2(mine[:, -1, 0] - 13.0)[:, None, None, :]
    return jnp.einsum(
        "pft,fpsr->str",
        jnp.asarray(transform_matrix(total)),
        mine,
        precision=lax.Precision.HIGHEST,
    )


def solution(mesh):
    fine = Mesh(mesh.devices.reshape(ZQ, ZR, NX, ZH, NY, NC), BLK + FREQ)
    return jax.shard_map(
        per_device,
        mesh=fine,
        in_specs=(
            P(None, FREQ, None, BLK),
            P(None, FREQ, None, BLK),
            P(FREQ, None, BLK),
        ),
        out_specs=P(FREQ, None, BLK),
        check_vma=False,
    )
```
